32 devices in a mesh: seq: 4 (over y, x), exp: 4 (over z), ffn: 2 (over core).
Axes of the slice: x: 2, y: 2, z: 4, core: 2. Of those that a mesh axis runs over, the one named last changes fastest.
Arguments:
- tokens: bfloat16 [8, 512, 768], P(('seq', 'ffn'), 'exp'), may hold values from -6 to 6
- route_ids: int32 [8, 512, 2], P(('seq', 'ffn'), 'exp'), may hold values from 0 to 15, all different within a row; in each aligned block of 128 rows (0 to 127, 128 to 255, ..., all dimensions but the last counted through in order) at most 32 rows name the same one
- w_query: bfloat16 [768, 768], P(('seq', 'exp', 'ffn')), may hold values from -0.21875 to 0.21875
- w_key: bfloat16 [768, 768], P(('seq', 'exp', 'ffn')), may hold values from -0.21875 to 0.21875
- w_value: bfloat16 [768, 768], P(('seq', 'exp', 'ffn')), may hold values from -0.21875 to 0.21875
- w_output: bfloat16 [768, 768], P(('seq', 'exp', 'ffn')), may hold values from -1.25 to 1.25
- norm_gains: bfloat16 [2, 768], P(None, ('seq', 'exp', 'ffn')), may hold values from 0.5 to 1.5
- rel_bias: bfloat16 [384], P(('seq', 'exp', 'ffn')), may hold values from -4 to 4
- router: bfloat16 [768, 16], P(('seq', 'exp', 'ffn')), may hold values from -0.21875 to 0.21875
- w_in: bfloat16 [16, 768, 3072], P(('seq', 'exp'), None, 'ffn'), may hold values from -0.21875 to 0.21875
- w_out: bfloat16 [16, 3072, 768], P(('seq', 'exp'), 'ffn'), may hold values from -0.109375 to 0.109375
- cotangent: bfloat16 [8, 512, 768], P(('seq', 'ffn'), 'exp'), may hold values from -6 to 6
Outputs:
- output: bfloat16 [8, 512, 768], P(('seq', 'ffn'), 'exp')
- grad_tokens: float32 [8, 512, 768], P(('seq', 'ffn'), 'exp')
- grad_w_query: float32 [768, 768], P(('seq', 'exp', 'ffn'))
- grad_w_key: float32 [768, 768], P(('seq', 'exp', 'ffn'))
- grad_w_value: float32 [768, 768], P(('seq', 'exp', 'ffn'))
- grad_w_output: float32 [768, 768], P(('seq', 'exp', 'ffn'))
- grad_norm_gains: float32 [2, 768], P(None, ('seq', 'exp', 'ffn'))
- grad_rel_bias: float32 [384], P(('seq', 'exp', 'ffn'))
- grad_router: float32 [768, 16], P(('seq', 'exp', 'ffn'))
- grad_w_in: float32 [16, 768, 3072], P(('seq', 'exp'), None, 'ffn')
- grad_w_out: float32 [16, 3072, 768], P(('seq', 'exp'), 'ffn')
The draws below stay inside these ranges and needn't reach their ends.
Inputs may be any that keep to these rules, and one draw needn't show every extreme that they name: `route_ids`: each token names 2 different experts. Among the 128 tokens of one device (aligned blocks of 128 tokens of a sequence) no expert is named more than 32 times, a bound that some block reaches.
All inputs are finite; a program needn't handle non-finite values.
Results may differ from the reference program's by a relative error of at most 0.015.
Values may be sent and summed in bfloat16 or wider, within the bound.
No kernel may reach another device: no remote copies, remote signals or barrier semaphores. Data moves between devices by JAX's collectives and lax.ppermute only.
A program may use at most 192 MiB of HBM per device.

```python
import math
import jax
import jax.numpy as jnp
import numpy as np
from jax import lax

D = 768
H = 12
HD = 64
FF = 3072
TOPK = 2
BUCKETS = 32
TOK = 128
EXPERTS = 16
SEQ_LEN = 512
SEQS = 8
CAP = 32


def block_levels(stream_key, dims, split, least, top_value):
    loudness = 1.0
    for position, parts in split:
        steps = jax.random.uniform(jax.random.fold_in(jax.random.fold_in(stream_key, 6), position), (parts,), jnp.float32, least / len(split), top_value / len(split))
        loudness = loudness * jnp.repeat(jnp.exp(steps), dims[position] // parts).reshape((-1,) + (1,) * (len(dims) - 1 - position))
    return loudness


def assign_block(stream_key, own, number, rows, amount, top, reach, lean):
    order = jax.random.permutation(stream_key, amount)
    crowded, ordinary = portions_of(amount, rows * top, reach, lean, True), portions_of(amount, rows * top, reach, lean, False)
    places = jnp.arange(amount)

    def named(lengths, offset_by):
        used = int((lengths > 0).sum())
        fixed = max(1, used // 4)
        passed = fixed + (places - fixed + offset_by * (used - fixed)) % max(1, amount - fixed)
        return jnp.zeros((amount,), jnp.int32).at[order[jnp.where(places < fixed, places, passed)]].set(jnp.asarray(lengths, jnp.int32))

    lengths = jnp.where(number % 4 == 0, named(crowded, number // 4), named(ordinary, number - number // 4 - 1))
    mixed = jax.random.permutation(jax.random.fold_in(own, 3), amount)
    donor, taker = mixed[0:amount // 2 * 2:2], mixed[1:amount // 2 * 2:2]
    slack = jnp.minimum(lengths[donor] - 1, reach - lengths[taker]) // 2
    slack = jnp.where((donor == order[0]) | (taker == order[0]) | (lengths[taker] == 0), 0, jnp.maximum(slack, 0))
    passed = jax.random.randint(jax.random.fold_in(own, 4), (amount // 2,), 0, 1 << 20) % (slack + 1)
    lengths = lengths.at[donor].add(-passed).at[taker].add(passed)
    members = jnp.searchsorted(jnp.cumsum(lengths), jnp.arange(rows * top), side="right").astype(jnp.int32)
    grid = members.reshape(top, rows).T
    grid = grid[jax.random.permutation(jax.random.fold_in(own, 1), rows)]
    offset_by = jax.random.randint(jax.random.fold_in(own, 2), (rows, 1), 0, top)
    return jnp.take_along_axis(grid, (jnp.arange(top)[None, :] + offset_by) % top, axis=1)


def portions_of(count, total, most, lean, full):
    loads = [(1 << 20) // math.isqrt(rank ** lean) + 1 for rank in range(1, count + 1)]
    largest = most if full else min(most, max(-(-total // count), total * loads[0] // sum(loads)))
    least = 1 if total - largest >= count - 1 else 0
    holding, spare = [largest] + [least] * (count - 1), total - largest - least * (count - 1)
    while spare > 0:
        free = [i for i in range(1, count) if holding[i] < largest] or [i for i in range(1, count) if holding[i] < most]
        mass, left = sum([loads[i] for i in free]), spare
        for i in free:
            more = min(most - holding[i], max(1, left * loads[i] // mass), spare)
            holding[i] = holding[i] + more
            spare = spare - more
    return np.array(holding)


def normal_values(own_key, dims, spread, limit, shards=(), kind=jnp.bfloat16):
    level = block_levels(own_key, dims, shards, -0.22, 0.18) if shards else 1.0
    drawn = jax.random.normal(own_key, dims, jnp.float32) * spread * level
    return jnp.minimum(jnp.maximum(drawn, -limit), limit).astype(kind)


def setup_inputs(seed: int = 0) -> dict:
    seeds = jax.random.split(jax.random.key(seed), 13)
    tokens = normal_values(seeds[0], (SEQS, SEQ_LEN, D), 1.0, 6.0, ((0, 8), (1, 4)))
    route_ids_keys = jax.random.split(jax.random.fold_in(seeds[1], 1), SEQS * SEQ_LEN // TOK)
    route_ids_turns = jax.random.permutation(jax.random.fold_in(seeds[1], 3), SEQS * SEQ_LEN // TOK)
    route_ids = jax.vmap(lambda own, number: assign_block(jax.random.fold_in(seeds[1], 2), own, number, TOK, EXPERTS, TOPK, CAP, 2))(route_ids_keys, route_ids_turns).reshape((SEQS, SEQ_LEN, TOPK))
    w_query = normal_values(seeds[2], (D, D), D ** -0.5, 0.21875, ((0, 32),))
    w_key = normal_values(seeds[3], (D, D), D ** -0.5, 0.21875, ((0, 32),))
    w_value = normal_values(seeds[4], (D, D), D ** -0.5, 0.21875, ((0, 32),))
    w_output = normal_values(seeds[5], (D, D), (D // 32) ** -0.5, 1.25, ((0, 32),))
    norm_gains = jnp.clip(1.0 + 0.1 * jax.random.normal(seeds[6], (2, D), jnp.float32), 0.5, 1.5).astype(jnp.bfloat16)
    rel_bias = normal_values(seeds[7], (H * BUCKETS,), 1.0, 4.0, ((0, 32),))
    router = normal_values(seeds[8], (D, EXPERTS), D ** -0.5, 0.21875, ((0, 32),))
    w_in = normal_values(seeds[9], (EXPERTS, D, FF), D ** -0.5, 0.21875, ((0, 16), (2, 2)))
    w_out = normal_values(seeds[10], (EXPERTS, FF, D), FF ** -0.5, 0.109375, ((0, 16), (1, 2)))
    cotangent = normal_values(seeds[11], (SEQS, SEQ_LEN, D), 1.0, 6.0, ((0, 8), (1, 4)))
    return dict(tokens=tokens, route_ids=route_ids, w_query=w_query, w_key=w_key, w_value=w_value, w_output=w_output, norm_gains=norm_gains, rel_bias=rel_bias, router=router, w_in=w_in, w_out=w_out, cotangent=cotangent)


bucket_edges = list(range(17)) + [math.ceil(16 * 8 ** ((bucket_level - 16) / 16)) for bucket_level in range(17, 32)]
epsilon = 1e-06

def rounded(values_in):
    return lax.optimization_barrier(values_in.astype(jnp.bfloat16)).astype(jnp.float32)

def matmul(left, right):
    return jnp.dot(left, right, preferred_element_type=jnp.float32)

def rms_forward(hidden, gain_row):
    factor = lax.rsqrt(lax.optimization_barrier(jnp.mean(hidden * hidden, axis=1, keepdims=True)) + epsilon)
    normed = hidden * factor
    return (normed, factor, normed * gain_row)

def rms_backward(grad_out, normed, factor, gain_row):
    grad_normed = grad_out * gain_row
    grad_hidden = factor * (grad_normed - normed * lax.optimization_barrier(jnp.mean(grad_normed * normed, axis=1, keepdims=True)))
    return (grad_hidden, lax.optimization_barrier(jnp.sum(grad_out * normed, axis=0)))

def gelu(pre_act):
    return 0.5 * pre_act * (1.0 + lax.erf(pre_act * 0.7071067811865476))

def gelu_slope(pre_act):
    return 0.5 * (1.0 + lax.erf(pre_act * 0.7071067811865476)) + pre_act * jnp.exp(-0.5 * pre_act * pre_act) * 0.3989422804014327

def reference_buckets(distance, length):
    spans = jnp.arange(length, dtype=jnp.int32)
    edges = jnp.array(bucket_edges, jnp.int32)
    per_distance = lax.optimization_barrier(jnp.sum((spans[None, :] >= edges[:, None]).astype(jnp.int32), axis=0)) - 1
    return per_distance[jnp.clip(distance, 0, length - 1)]

def bucket_sums(flat_scores, flat_buckets):
    return jax.ops.segment_sum(flat_scores, flat_buckets, num_segments=BUCKETS)

def block_scores(query, key_full, table, first, length, block):
    factor = HD ** (-0.5)
    query_block = lax.dynamic_slice_in_dim(query, first, block, 0).astype(jnp.float32)
    distance = (first + jnp.arange(block, dtype=jnp.int32))[:, None] - jnp.arange(length, dtype=jnp.int32)[None, :]
    bucket = reference_buckets(distance, length)
    scores = jnp.einsum('qhd,khd->hqk', query_block, key_full) * factor + table[:, bucket]
    return (query_block, scores, distance[None] >= 0, bucket)

def attention_forward(query, key, value, table):
    length = query.shape[0]
    block = min(512, length)
    key_full = key.astype(jnp.float32)
    value_full = value.astype(jnp.float32)

    def one_block(number):
        query_block, scores, causal, bucket = block_scores(query, key_full, table, number * block, length, block)
        weights = jnp.where(causal, jnp.exp(scores), 0.0)
        total = lax.optimization_barrier(jnp.sum(weights, axis=2)).T
        numerator = jnp.einsum('hqk,khd->qhd', rounded(weights), value_full)
        return ((numerator / total[:, :, None]).astype(jnp.bfloat16), jnp.log(total))
    attended, log_total = lax.map(one_block, jnp.arange(length // block, dtype=jnp.int32))
    return (attended.reshape(length, H, HD), log_total.reshape(length, H))

def attention_backward(query, key, value, table, attended, log_total, grad_heads):
    length = query.shape[0]
    block = min(512, length)
    factor = HD ** (-0.5)
    key_full = key.astype(jnp.float32)
    value_full = value.astype(jnp.float32)
    row_dots = lax.optimization_barrier(jnp.sum(grad_heads.astype(jnp.float32) * attended.astype(jnp.float32), axis=2))

    def advance(running, number):
        grad_keys, grad_values, grad_table = running
        first = number * block
        query_block, scores, causal, bucket = block_scores(query, key_full, table, first, length, block)
        grad_block = lax.dynamic_slice_in_dim(grad_heads, first, block, 0).astype(jnp.float32)
        total_block = lax.dynamic_slice_in_dim(log_total, first, block, 0)
        dots_block = lax.dynamic_slice_in_dim(row_dots, first, block, 0)
        probabilities = jnp.where(causal, jnp.exp(scores - total_block.T[:, :, None]), 0.0)
        grad_values = grad_values + jnp.einsum('hqk,qhd->khd', rounded(probabilities), grad_block)
        grad_probs = jnp.einsum('qhd,khd->hqk', grad_block, value_full)
        grad_scores = probabilities * (grad_probs - dots_block.T[:, :, None])
        low_grads = rounded(grad_scores)
        grad_query = jnp.einsum('hqk,khd->qhd', low_grads, key_full) * factor
        grad_keys = grad_keys + jnp.einsum('hqk,qhd->khd', low_grads, query_block) * factor
        grad_table = grad_table + jax.vmap(bucket_sums, in_axes=(0, None))(grad_scores.reshape(H, -1), bucket.reshape(-1))
        return ((grad_keys, grad_values, grad_table), grad_query)
    zeros_heads = jnp.zeros((length, H, HD), jnp.float32)
    start_state = (zeros_heads, zeros_heads, jnp.zeros((H, BUCKETS), jnp.float32))
    (grad_keys, grad_values, grad_table), grad_query = lax.scan(advance, start_state, jnp.arange(length // block, dtype=jnp.int32))
    return (grad_query.reshape(length, H, HD), grad_keys, grad_values, grad_table)

def expert_forward(operands):
    expert_rows, weight_in, weight_out = operands
    activated = gelu(matmul(expert_rows, weight_in)).astype(jnp.bfloat16)
    return matmul(activated, weight_out)

def expert_backward(operands):
    expert_rows, grad_rows, weight_in, weight_out = operands
    pre_act = matmul(expert_rows, weight_in)
    activated = gelu(pre_act).astype(jnp.bfloat16)
    grad_pre = (matmul(grad_rows, weight_out.T) * gelu_slope(pre_act)).astype(jnp.bfloat16)
    return (matmul(expert_rows.T, grad_pre), matmul(activated.T, grad_rows), matmul(grad_pre, weight_in.T))

def reference(tokens, route_ids, w_query, w_key, w_value, w_output, norm_gains, rel_bias, router, w_in, w_out, cotangent):
    table = rel_bias.astype(jnp.float32).reshape(H, BUCKETS)
    gains = norm_gains.astype(jnp.float32)
    flat_in = tokens.reshape(-1, D).astype(jnp.float32)
    normed_one, scale_one, scaled_one = rms_forward(flat_in, gains[0])
    input_normed = scaled_one.astype(jnp.bfloat16)
    query = matmul(input_normed, w_query).astype(jnp.bfloat16)
    key = matmul(input_normed, w_key).astype(jnp.bfloat16)
    value = matmul(input_normed, w_value).astype(jnp.bfloat16)
    attended_parts = []
    total_parts = []
    for sequence in range(SEQS):
        lower = sequence * SEQ_LEN
        upper = lower + SEQ_LEN
        attended_seq, total_seq = attention_forward(query[lower:upper].reshape(SEQ_LEN, H, HD), key[lower:upper].reshape(SEQ_LEN, H, HD), value[lower:upper].reshape(SEQ_LEN, H, HD), table)
        attended_parts.append(attended_seq)
        total_parts.append(total_seq)
    attended = jnp.concatenate(attended_parts, axis=0).reshape(-1, D)
    residual = flat_in + matmul(attended, w_output)
    normed_two, scale_two, scaled_two = rms_forward(residual, gains[1])
    moe_normed = scaled_two.astype(jnp.bfloat16)
    logits = matmul(moe_normed, router)
    expert_ids = route_ids.reshape(-1, TOPK)
    first_logit = jnp.take_along_axis(logits, expert_ids[:, 0:1], axis=1)[:, 0]
    second_logit = jnp.take_along_axis(logits, expert_ids[:, 1:2], axis=1)[:, 0]
    first_gate = jax.nn.sigmoid(first_logit - second_logit)
    gate_pair = jnp.stack([first_gate, 1.0 - first_gate], axis=1)
    block_count = SEQS * SEQ_LEN // TOK
    per_expert = block_count * CAP
    ids_block = expert_ids.reshape(block_count, TOK * TOPK)
    expert_range = jnp.arange(EXPERTS, dtype=jnp.int32)
    assign_hot = (ids_block[:, :, None] == expert_range[None, None, :]).astype(jnp.int32)
    slot_index = lax.optimization_barrier(jnp.sum(assign_hot * (jnp.cumsum(assign_hot, axis=1) - assign_hot), axis=2))
    target = (ids_block * per_expert + jnp.arange(block_count, dtype=jnp.int32)[:, None] * CAP + slot_index).reshape(-1)
    dispatched = jnp.zeros((EXPERTS * per_expert, D), jnp.bfloat16).at[target].set(jnp.repeat(moe_normed, TOPK, axis=0))
    dispatched = dispatched.reshape(EXPERTS, per_expert, D)
    expert_out = lax.map(expert_forward, (dispatched, w_in, w_out)).reshape(-1, D)
    picked = jnp.take(expert_out, target, axis=0).reshape(-1, TOPK, D)
    output = (residual + lax.optimization_barrier(jnp.sum(gate_pair[:, :, None] * picked, axis=1))).astype(jnp.bfloat16)
    grad_mix = cotangent.reshape(-1, D).astype(jnp.float32)
    grad_gate = lax.optimization_barrier(jnp.sum(grad_mix[:, None, :] * picked, axis=2))
    grad_picked = (gate_pair[:, :, None] * grad_mix[:, None, :]).astype(jnp.bfloat16).reshape(-1, D)
    grad_dispatched = jnp.zeros((EXPERTS * per_expert, D), jnp.bfloat16).at[target].set(grad_picked)
    grad_w_in, grad_w_out, grad_rows = lax.map(expert_backward, (dispatched, grad_dispatched.reshape(EXPERTS, per_expert, D), w_in, w_out))
    grad_normed_two = lax.optimization_barrier(jnp.sum(jnp.take(grad_rows.reshape(-1, D), target, axis=0).reshape(-1, TOPK, D), axis=1))
    gate_slope = (grad_gate[:, 0] - grad_gate[:, 1]) * first_gate * (1.0 - first_gate)
    first_hot = (expert_ids[:, 0:1] == expert_range[None, :]).astype(jnp.float32)
    second_hot = (expert_ids[:, 1:2] == expert_range[None, :]).astype(jnp.float32)
    grad_logits = (gate_slope[:, None] * (first_hot - second_hot)).astype(jnp.bfloat16)
    grad_router = matmul(moe_normed.T, grad_logits)
    grad_normed_two = grad_normed_two + matmul(grad_logits, router.T)
    grad_res_norm, grad_gain_two = rms_backward(grad_normed_two, normed_two, scale_two, gains[1])
    grad_residual = grad_mix + grad_res_norm
    grad_branch = grad_residual.astype(jnp.bfloat16)
    grad_w_output = matmul(attended.T, grad_branch)
    grad_attended = matmul(grad_branch, w_output.T).astype(jnp.bfloat16)
    query_parts = []
    key_parts = []
    value_parts = []
    grad_table = jnp.zeros((H, BUCKETS), jnp.float32)
    for sequence in range(SEQS):
        lower = sequence * SEQ_LEN
        upper = lower + SEQ_LEN
        grad_q_seq, grad_k_seq, grad_v_seq, table_seq = attention_backward(query[lower:upper].reshape(SEQ_LEN, H, HD), key[lower:upper].reshape(SEQ_LEN, H, HD), value[lower:upper].reshape(SEQ_LEN, H, HD), table, attended_parts[sequence], total_parts[sequence], grad_attended[lower:upper].reshape(SEQ_LEN, H, HD))
        query_parts.append(grad_q_seq)
        key_parts.append(grad_k_seq)
        value_parts.append(grad_v_seq)
        grad_table = grad_table + table_seq
    grad_query = jnp.concatenate(query_parts, axis=0).reshape(-1, D).astype(jnp.bfloat16)
    grad_key = jnp.concatenate(key_parts, axis=0).reshape(-1, D).astype(jnp.bfloat16)
    grad_value = jnp.concatenate(value_parts, axis=0).reshape(-1, D).astype(jnp.bfloat16)
    grad_w_query = matmul(input_normed.T, grad_query)
    grad_w_key = matmul(input_normed.T, grad_key)
    grad_w_value = matmul(input_normed.T, grad_value)
    grad_normed_one = matmul(grad_query, w_query.T) + matmul(grad_key, w_key.T) + matmul(grad_value, w_value.T)
    grad_in_norm, grad_gain_one = rms_backward(grad_normed_one, normed_one, scale_one, gains[0])
    grad_tokens = grad_residual + grad_in_norm
    return (output.reshape(tokens.shape), grad_tokens.reshape(tokens.shape), grad_w_query, grad_w_key, grad_w_value, grad_w_output, jnp.stack([grad_gain_one, grad_gain_two]), grad_table.reshape(-1), grad_router, grad_w_in, grad_w_out)
```

```python
import functools
import math

import jax
import jax.numpy as jnp
import numpy as np
from jax import lax
from jax.experimental import pallas as pl
from jax.experimental.pallas import tpu as pltpu
from jax.sharding import PartitionSpec as P

H = 12
HD = 64
TOPK = 2
BUCKETS = 32
LANES = 128

bucket_edges = list(range(17)) + [
    math.ceil(16 * 8 ** ((bucket_level - 16) / 16)) for bucket_level in range(17, 32)
]
epsilon = 1e-06
scale = HD ** (-0.5)
f32 = jnp.float32
bf16 = jnp.bfloat16
EXACT = lax.Precision.HIGHEST


def dot(left, right, left_dim=1, right_dim=0, precision=None):
    return lax.dot_general(
        left,
        right,
        (((left_dim,), (right_dim,)), ((), ())),
        precision=precision,
        preferred_element_type=f32,
    )


def mean_rows(values):
    return jnp.mean(values, axis=1, keepdims=True)


def iota(shape, axis):
    return lax.broadcasted_iota(jnp.int32, shape, axis)


def rms_factor(hidden):
    return lax.rsqrt(mean_rows(hidden * hidden) + epsilon)


def rms_backward(grad_out, normed, factor, gain_row):
    grad_normed = grad_out * gain_row
    return factor * (grad_normed - normed * mean_rows(grad_normed * normed))


def shear(tile, leftward):
    rows = iota(tile.shape, 0)
    for bit in range(7):
        step = 1 << bit
        moved = pltpu.roll(tile, LANES - step if leftward else step, axis=1)
        tile = jnp.where((rows & step) != 0, moved, tile)
    return tile


class Plan:
    def __init__(self, tok, width, hidden):
        self.seq = lax.axis_size("seq")
        self.exp = lax.axis_size("exp")
        self.ffn = lax.axis_size("ffn")
        self.experts = self.seq * self.exp
        self.devices = self.experts * self.ffn
        self.tok = tok
        self.width = width
        self.hidden = hidden
        self.groups = math.gcd(H, self.exp)
        self.copies = self.exp // self.groups
        self.gh = H // self.groups
        self.gw = self.gh * HD
        self.length = self.exp * tok
        self.queries = self.length // self.copies
        self.blocks = self.exp // self.copies
        self.cap = 2 * tok * TOPK // self.experts
        self.slots = self.experts * self.cap
        self.shard = width // self.devices
        self.bias_shard = H * BUCKETS // self.devices
        self.extra = self.experts + 3
        self.qkv = 3 * self.gw
        self.packed = -(-(self.qkv + self.extra) // LANES) * LANES
        self.chunk = LANES * max(1, -(-(2 * self.extra) // LANES))
        self.first = self.packed - self.chunk
        self.off = self.qkv - self.first
        assert self.first % self.chunk == 0 and 0 <= self.off
        assert self.off + self.extra <= self.chunk
        assert tok == LANES and bucket_edges[-1] <= LANES

    def selectors(self):
        head = np.zeros((16, self.width), np.float32)
        spread = np.zeros((self.width, LANES), np.float32)
        distance = (-np.arange(LANES)) % LANES
        bucket = (distance[:, None] >= np.array(bucket_edges)[None, :]).sum(1) - 1
        for device in range(self.devices):
            for place in range(self.bias_shard):
                row = device * self.shard + place
                flat = device * self.bias_shard + place
                head[flat // BUCKETS, row] = 1.0
                spread[row] = bucket == flat % BUCKETS
        return jnp.asarray(head, bf16), jnp.asarray(spread, bf16)


def whole(shape, memory_space=pltpu.VMEM):
    zeros = (0,) * len(shape)
    return pl.BlockSpec(shape, lambda step: zeros, memory_space=memory_space)


def chunk_spec(plan):
    index = plan.first // plan.chunk
    return pl.BlockSpec((plan.width, plan.chunk), lambda step: (0, index), memory_space=pltpu.VMEM)


def bias_tile(table_ref, head):
    row = table_ref[pl.ds(head, 1), :]
    far = row[:, 1:2]
    return shear(jnp.broadcast_to(row, (LANES, LANES)), False), far


def score_rows(plan, qkv_ref, head, query, base, keys, tile, far):
    lanes = head * HD
    query_rows = qkv_ref[pl.ds(query, LANES), lanes : lanes + HD]
    key_rows = qkv_ref[0:keys, plan.gw + lanes : plan.gw + lanes + HD]
    value_rows = qkv_ref[0:keys, 2 * plan.gw + lanes : 2 * plan.gw + lanes + HD]
    distance = base + iota((LANES, keys), 0) - iota((LANES, keys), 1)
    bias = jnp.where(distance >= LANES, far, jnp.concatenate([tile] * (keys // LANES), axis=1))
    scores = dot(query_rows, key_rows, 1, 1) * scale + bias
    return scores, distance, query_rows, key_rows, value_rows


def first_query(plan):
    if plan.copies == 1:
        return 0
    return (lax.axis_index("exp") % plan.copies) * plan.queries


def first_head(plan):
    return (lax.axis_index("exp") // plan.copies) * plan.gh


def query_blocks(plan):
    start = first_query(plan)
    for block in range(plan.blocks):
        local = block * LANES
        keys = local + LANES if plan.copies == 1 else plan.length
        at = start + local
        if plan.copies > 1:
            at = pl.multiple_of(at, LANES)
        yield local, at, keys


def attend_kernel(plan, x_ref, wp_ref, head_ref, spread_ref, att_ref, qkv_ref, lse_ref, table_ref):
    extra = wp_ref[:, plan.first : plan.packed].astype(f32)
    place = plan.off + plan.experts
    gain = jnp.transpose(extra)[place : place + 1, :]
    bias_column = extra[:, place + 2 : place + 3]
    table_ref[...] = dot(head_ref[...], (bias_column * spread_ref[...].astype(f32)).astype(bf16))
    hidden = x_ref[...].astype(f32)
    normed = hidden * rms_factor(hidden)
    scaled = (normed * gain).astype(bf16)
    qkv_ref[...] = dot(scaled, wp_ref[:, 0 : plan.qkv]).astype(bf16)
    lse_ref[...] = jnp.zeros_like(lse_ref)
    for head in range(plan.gh):
        tile, far = bias_tile(table_ref, first_head(plan) + head)
        for local, at, keys in query_blocks(plan):
            scores, distance, _, _, value_rows = score_rows(
                plan, qkv_ref, head, at, at, keys, tile, far
            )
            weights = jnp.where(distance >= 0, jnp.exp(scores), 0.0)
            total = jnp.sum(weights, axis=1, keepdims=True)
            numerator = dot(weights.astype(bf16), value_rows)
            att_ref[local : local + LANES, head * HD : (head + 1) * HD] = (
                numerator / total
            ).astype(bf16)
            lse_ref[local : local + LANES, head : head + 1] = jnp.log(total)


def routing(plan, ids_ref):
    lane = iota((plan.tok, plan.chunk), 1) - plan.off
    first_hot = lane == ids_ref[:, 0:1]
    second_hot = lane == ids_ref[:, 1:2]
    return first_hot, second_hot


def pick(hot, values):
    return jnp.sum(jnp.where(hot, values, 0.0), axis=1, keepdims=True)


def placements(plan, meta):
    slot = iota((plan.tok, plan.slots), 1).astype(f32)
    return (
        (slot == meta[:, 1:2]).astype(f32).astype(bf16),
        (slot == meta[:, 2:3]).astype(f32).astype(bf16),
    )


def middle_kernel(
    plan, att_ref, wo_ref, x_ref, cot_ref, ids_ref, chunk_ref, send_ref, res_ref, meta_ref, atok_ref
):
    for group in range(plan.groups):
        atok_ref[:, group * plan.gw : (group + 1) * plan.gw] = att_ref[group]
    residual = x_ref[...].astype(f32) + dot(atok_ref[...], wo_ref[...])
    res_ref[...] = residual
    chunk = chunk_ref[...]
    place = plan.off + plan.experts + 1
    gain = jnp.transpose(chunk.astype(f32))[place : place + 1, :]
    normed = residual * rms_factor(residual)
    moe_normed = (normed * gain).astype(bf16)
    logits = dot(moe_normed, chunk)
    first_hot, second_hot = routing(plan, ids_ref)
    margin = pick(first_hot, logits) - pick(second_hot, logits)
    first_gate = 1.0 / (1.0 + jnp.exp(-margin))
    named = jnp.logical_or(first_hot, second_hot).astype(f32).astype(bf16)
    earlier = (iota((plan.tok, plan.tok), 0) > iota((plan.tok, plan.tok), 1)).astype(f32)
    counts = dot(earlier.astype(bf16), named)
    ids = ids_ref[...].astype(f32) * float(plan.cap)
    meta_lane = iota((plan.tok, LANES), 1)
    meta = jnp.where(
        meta_lane == 0,
        first_gate,
        jnp.where(
            meta_lane == 1,
            ids[:, 0:1] + pick(first_hot, counts),
            jnp.where(meta_lane == 2, ids[:, 1:2] + pick(second_hot, counts), 0.0),
        ),
    )
    meta_ref[...] = meta
    first_place, second_place = placements(plan, meta)
    cot = cot_ref[...].astype(f32)
    first_grad = (first_gate * cot).astype(bf16)
    second_grad = ((1.0 - first_gate) * cot).astype(bf16)
    send_ref[:, 0 : plan.width] = dot(first_place + second_place, moe_normed, 0, 0).astype(bf16)
    send_ref[:, plan.width :] = (
        dot(first_place, first_grad, 0, 0) + dot(second_place, second_grad, 0, 0)
    ).astype(bf16)


def expert_kernel(
    plan, own_ref, other_ref, win_ref, wout_ref, mine_ref, theirs_ref, gin_ref, gout_ref, rows_ref, acc_ref
):
    step = pl.program_id(0)
    half = own_ref.shape[0]
    width = plan.width

    @pl.when(step == 0)
    def _():
        rows_ref[0:half, :] = own_ref[...]
        rows_ref[half:, :] = other_ref[...]
        acc_ref[...] = jnp.zeros_like(acc_ref)

    rows = rows_ref[:, 0:width]
    grads = rows_ref[:, width:]
    w_in = win_ref[0]
    w_out = wout_ref[0]
    pre_act = dot(rows, w_in)
    phi = 0.5 * (1.0 + lax.erf(pre_act * 0.7071067811865476))
    activated = (pre_act * phi).astype(bf16)
    slope = phi + pre_act * jnp.exp(-0.5 * pre_act * pre_act) * 0.3989422804014327
    grad_pre = (dot(grads, w_out, 1, 1) * slope).astype(bf16)
    acc_ref[:, 0:width] += dot(activated, w_out)
    acc_ref[:, width:] += dot(grad_pre, w_in, 1, 1)
    gout_ref[0] = dot(activated, grads, 0, 0)
    gin_ref[0] = dot(rows, grad_pre, 0, 0)

    @pl.when(step == pl.num_programs(0) - 1)
    def _():
        mine_ref[...] = acc_ref[0:half, :]
        theirs_ref[...] = acc_ref[half:, :].astype(bf16)


def combine_kernel(
    plan, back_ref, meta_ref, res_ref, cot_ref, ids_ref, chunk_ref, wo_ref, atok_ref,
    out_ref, gres_ref, gatt_ref, gwo_ref, small_ref,
):
    width = plan.width
    meta = meta_ref[...]
    first_gate = meta[:, 0:1]
    first_place, second_place = placements(plan, meta)
    back = back_ref[...]
    first = dot(first_place, back)
    second = dot(second_place, back)
    residual = res_ref[...]
    out_ref[...] = (
        residual + (first_gate * first[:, 0:width] + (1.0 - first_gate) * second[:, 0:width])
    ).astype(bf16)
    cot = cot_ref[...].astype(f32)
    grad_gate = jnp.sum(cot * first[:, 0:width], axis=1, keepdims=True) - jnp.sum(
        cot * second[:, 0:width], axis=1, keepdims=True
    )
    gate_slope = grad_gate * first_gate * (1.0 - first_gate)
    first_hot, second_hot = routing(plan, ids_ref)
    grad_logits = (
        gate_slope * (first_hot.astype(f32) - second_hot.astype(f32))
    ).astype(bf16)
    chunk = chunk_ref[...]
    place = plan.off + plan.experts + 1
    gain = jnp.transpose(chunk.astype(f32))[place : place + 1, :]
    factor = rms_factor(residual)
    normed = residual * factor
    moe_normed = (normed * gain).astype(bf16)
    grad_normed = first[:, width:] + second[:, width:] + dot(grad_logits, chunk, 1, 1)
    grad_residual = cot + rms_backward(grad_normed, normed, factor, gain)
    gres_ref[...] = grad_residual
    grad_branch = grad_residual.astype(bf16)
    grad_attended = dot(grad_branch, wo_ref[...], 1, 1).astype(bf16)
    for group in range(plan.groups):
        gatt_ref[group] = grad_attended[:, group * plan.gw : (group + 1) * plan.gw]
    gwo_ref[...] = dot(atok_ref[...], grad_branch, 0, 0).astype(bf16)
    grad_router = dot(moe_normed, grad_logits, 0, 0)
    grad_gain = jnp.sum(grad_normed * normed, axis=0, keepdims=True)
    columns = jnp.transpose(jnp.broadcast_to(grad_gain, (plan.chunk, width)))
    lane = iota((width, plan.chunk), 1)
    small_ref[...] = jnp.where(
        lane == place, columns, jnp.where(lane < plan.off, 0.0, grad_router)
    )


def backward_kernel(
    plan, x_ref, wp_ref, head_ref, spread_ref, qkv_ref, att_ref, gatt_ref, lse_ref, table_ref, part_ref,
    gx_ref, gw_ref, small_ref, pair_ref, grad_ref, sums_ref,
):
    extra = wp_ref[:, plan.first : plan.packed].astype(f32)
    place = plan.off + plan.experts
    gain = jnp.transpose(extra)[place : place + 1, :]
    pair_ref[...] = jnp.zeros_like(pair_ref)
    sums_ref[...] = jnp.zeros_like(sums_ref)
    if plan.copies > 1:
        grad_ref[...] = jnp.zeros_like(grad_ref)
    for head in range(plan.gh):
        lanes = head * HD
        tile, far = bias_tile(table_ref, first_head(plan) + head)
        near_sum = jnp.zeros((LANES, LANES), f32)
        far_sum = jnp.zeros((1, LANES), f32)
        for local, at, keys in query_blocks(plan):
            scores, distance, query_rows, key_rows, value_rows = score_rows(
                plan, qkv_ref, head, at, at, keys, tile, far
            )
            log_total = lse_ref[local : local + LANES, head : head + 1]
            weights = jnp.where(distance >= 0, jnp.exp(scores - log_total), 0.0)
            grads = gatt_ref[local : local + LANES, lanes : lanes + HD]
            attended = att_ref[local : local + LANES, lanes : lanes + HD]
            row_dots = jnp.sum(grads.astype(f32) * attended.astype(f32), axis=1, keepdims=True)
            grad_scores = weights * (dot(grads, value_rows, 1, 1) - row_dots)
            low = grad_scores.astype(bf16)
            near = jnp.where(distance < LANES, grad_scores, 0.0)
            rest = jnp.sum(jnp.where(distance < LANES, 0.0, grad_scores), axis=0, keepdims=True)
            for part in range(keys // LANES):
                near_sum = near_sum + near[:, part * LANES : (part + 1) * LANES]
                far_sum = far_sum + rest[:, part * LANES : (part + 1) * LANES]
            grad_ref[pl.ds(at, LANES), lanes : lanes + HD] = (dot(low, key_rows) * scale).astype(
                bf16
            )
            pair_ref[0:keys, lanes : lanes + HD] += dot(low, query_rows, 0, 0) * scale
            pair_ref[0:keys, plan.gw + lanes : plan.gw + lanes + HD] += dot(
                weights.astype(bf16), grads, 0, 0
            )
        by_distance = jnp.sum(shear(near_sum, True), axis=0, keepdims=True)
        by_distance = by_distance + jnp.where(
            iota((1, LANES), 1) == 1, jnp.sum(far_sum, axis=1, keepdims=True), 0.0
        )
        sums_ref[pl.ds(first_head(plan) + head, 1), :] = by_distance
    grad_ref[:, plan.gw :] = pair_ref[...].astype(bf16)
    hidden = x_ref[...].astype(f32)
    normed = hidden * rms_factor(hidden)
    scaled = (normed * gain).astype(bf16)
    grads = grad_ref[...]
    gw_ref[...] = dot(scaled, grads, 0, 0).astype(bf16)
    grad_normed = dot(grads, wp_ref[:, 0 : plan.qkv], 1, 1)
    for block in range(plan.exp):
        gx_ref[block] = grad_normed[block * plan.tok : (block + 1) * plan.tok].astype(bf16)
    grad_gain = jnp.sum(grad_normed * normed, axis=0, keepdims=True)
    columns = jnp.transpose(jnp.broadcast_to(grad_gain, (plan.chunk, plan.width)))
    by_row = dot(head_ref[...].astype(f32), sums_ref[...], 0, 0, EXACT)
    bias_column = jnp.sum(by_row * spread_ref[...].astype(f32), axis=1, keepdims=True)
    lane = iota((plan.width, plan.chunk), 1)
    small = part_ref[...] + jnp.where(
        lane == place, columns, jnp.where(lane == place + 2, bias_column, 0.0)
    )
    if plan.off:
        small = pltpu.roll(small, plan.chunk - plan.off, axis=1)
    high = small.astype(bf16).astype(f32)
    low = pltpu.roll(small - high, plan.extra, axis=1)
    small_ref[...] = jnp.where(lane < plan.extra, high, low).astype(bf16)


def finish_kernel(plan, gx_ref, gres_ref, x_ref, chunk_ref, out_ref):
    place = plan.off + plan.experts
    gain = jnp.transpose(chunk_ref[...].astype(f32))[place : place + 1, :]
    grad_normed = gx_ref[0].astype(f32)
    for block in range(1, plan.exp):
        grad_normed = grad_normed + gx_ref[block].astype(f32)
    hidden = x_ref[...].astype(f32)
    factor = rms_factor(hidden)
    out_ref[...] = gres_ref[...] + rms_backward(grad_normed, hidden * factor, factor, gain)


def unpack_kernel(plan, got_ref, gq_ref, gk_ref, gv_ref, gwo_ref, small_ref):
    by_exp = []
    for place in range(plan.exp):
        total = got_ref[place].astype(f32)
        for row in range(1, plan.seq):
            total = total + got_ref[row * plan.exp + place].astype(f32)
        by_exp.append(total)
    joined = by_exp[0]
    for total in by_exp[1:]:
        joined = joined + total
    gwo_ref[...] = joined[:, 0 : plan.width]
    small = joined[:, plan.width : plan.width + plan.chunk]
    small_ref[...] = small + pltpu.roll(small, plan.chunk - plan.extra, axis=1)
    start = plan.width + plan.chunk
    for group in range(plan.groups):
        total = by_exp[group * plan.copies]
        for copy in range(1, plan.copies):
            total = total + by_exp[group * plan.copies + copy]
        for number, ref in enumerate((gq_ref, gk_ref, gv_ref)):
            at = start + number * plan.gw
            ref[:, group * plan.gw : (group + 1) * plan.gw] = total[:, at : at + plan.gw]


def call(kernel, plan, in_specs, out, scratch=(), name=None):
    return pl.pallas_call(
        functools.partial(kernel, plan),
        grid=(1,),
        in_specs=in_specs,
        out_specs=[whole(o.shape) for o in out],
        out_shape=out,
        scratch_shapes=list(scratch),
        name=name,
    )


def shaped(*dims, dtype=bf16):
    return jax.ShapeDtypeStruct(dims, dtype)


def body(
    tokens, route_ids, w_query, w_key, w_value, w_output, norm_gains, rel_bias, router,
    w_in, w_out, cotangent,
):
    tok, width = tokens.shape[1:]
    hidden = w_in.shape[2]
    plan = Plan(tok, width, hidden)
    experts = plan.experts
    grid_axes = ("seq", "exp")
    ffn_index = lax.axis_index("ffn")
    swap = [(core, plan.ffn - 1 - core) for core in range(plan.ffn)]

    def exchange(values):
        return lax.all_to_all(values, grid_axes, split_axis=0, concat_axis=0, tiled=True)

    def along(values):
        return lax.all_to_all(values, "exp", split_axis=0, concat_axis=0, tiled=True)

    def partner(values):
        return lax.ppermute(values, "ffn", swap)

    def both_cores(values):
        other = partner(values)
        return jnp.where(
            ffn_index == 0,
            jnp.stack([values, other], axis=1),
            jnp.stack([other, values], axis=1),
        )

    x = tokens[0]
    cot = cotangent[0]
    ids = route_ids[0]
    shard = plan.shard
    bias_column = jnp.pad(rel_bias, (0, shard - plan.bias_shard))[:, None]
    by_group = [
        jnp.transpose(w.reshape(shard, plan.groups, plan.gw), (1, 0, 2))
        for w in (w_query, w_key, w_value)
    ]
    extra = jnp.concatenate([router, norm_gains.T, bias_column], axis=1)
    extra = jnp.pad(extra, ((0, 0), (0, plan.packed - plan.qkv - plan.extra)))
    packed = jnp.concatenate(
        by_group + [jnp.broadcast_to(extra[None], (plan.groups,) + extra.shape)], axis=2
    )
    packed = jnp.broadcast_to(
        packed[None, :, None], (plan.seq, plan.groups, plan.copies, shard, plan.packed)
    ).reshape(experts, shard, plan.packed)
    x_all = along(jnp.broadcast_to(x[None], (plan.exp, tok, width))).reshape(plan.length, width)
    wp = both_cores(exchange(packed)).reshape(width, plan.packed)
    wo = both_cores(
        exchange(jnp.broadcast_to(w_output[None], (experts, shard, width)))
    ).reshape(width, width)
    head_rows, spread = plan.selectors()

    att, qkv, lse, table = call(
        attend_kernel,
        plan,
        [whole(x_all.shape), whole(wp.shape), whole(head_rows.shape), whole(spread.shape)],
        [
            shaped(plan.queries, plan.gw),
            shaped(plan.length, plan.qkv),
            shaped(plan.queries, LANES, dtype=f32),
            shaped(16, LANES, dtype=f32),
        ],
        name="attend",
    )(x_all, wp, head_rows, spread)

    def to_owners(rows):
        blocks = rows.reshape(plan.blocks, tok, plan.gw)
        if plan.copies == 1:
            return blocks
        copy = lax.axis_index("exp") % plan.copies
        mine = jnp.arange(plan.copies) == copy
        return jnp.where(mine[:, None, None, None], blocks[None], 0).reshape(
            plan.exp, tok, plan.gw
        )

    att_recv = along(to_owners(att))
    if plan.copies > 1:
        att_recv = jnp.sum(att_recv.reshape(plan.groups, plan.copies, tok, plan.gw), axis=1)

    send, residual, meta, atok = call(
        middle_kernel,
        plan,
        [
            whole(att_recv.shape), whole(wo.shape), whole(x.shape), whole(cot.shape),
            whole(ids.shape), chunk_spec(plan),
        ],
        [
            shaped(plan.slots, 2 * width),
            shaped(tok, width, dtype=f32),
            shaped(tok, LANES, dtype=f32),
            shaped(tok, width),
        ],
        name="middle",
    )(att_recv, wo, x, cot, ids, wp)

    own = exchange(send.reshape(experts, plan.cap, 2 * width)).reshape(plan.slots, 2 * width)
    other = partner(own)
    block = 512 if hidden % 512 == 0 else hidden
    row_spec = pl.BlockSpec((plan.slots, 2 * width), lambda step: (0, 0))
    in_spec = pl.BlockSpec((1, width, block), lambda step: (0, 0, step))
    out_spec = pl.BlockSpec((1, block, width), lambda step: (0, step, 0))
    mine, theirs, grad_w_in, grad_w_out = pl.pallas_call(
        functools.partial(expert_kernel, plan),
        grid=(hidden // block,),
        in_specs=[row_spec, row_spec, in_spec, out_spec],
        out_specs=[row_spec, row_spec, in_spec, out_spec],
        out_shape=[
            shaped(plan.slots, 2 * width, dtype=f32),
            shaped(plan.slots, 2 * width),
            shaped(1, width, hidden, dtype=f32),
            shaped(1, hidden, width, dtype=f32),
        ],
        scratch_shapes=[
            pltpu.VMEM((2 * plan.slots, 2 * width), bf16),
            pltpu.VMEM((2 * plan.slots, 2 * width), f32),
        ],
        name="experts",
    )(own, other, w_in, w_out)
    total = (mine + partner(theirs).astype(f32)).astype(bf16)
    back = exchange(total.reshape(experts, plan.cap, 2 * width)).reshape(plan.slots, 2 * width)

    output, grad_residual, gatt, gwo, part = call(
        combine_kernel,
        plan,
        [
            whole(back.shape), whole(meta.shape), whole(residual.shape), whole(cot.shape),
            whole(ids.shape), chunk_spec(plan), whole(wo.shape), whole(atok.shape),
        ],
        [
            shaped(tok, width),
            shaped(tok, width, dtype=f32),
            shaped(plan.groups, tok, plan.gw),
            shaped(width, width),
            shaped(width, plan.chunk, dtype=f32),
        ],
        name="combine",
    )(back, meta, residual, cot, ids, wp, wo, atok)

    if plan.copies > 1:
        gatt = jnp.broadcast_to(
            gatt[:, None], (plan.groups, plan.copies, tok, plan.gw)
        ).reshape(plan.exp, tok, plan.gw)
    gatt_recv = along(gatt)
    if plan.copies > 1:
        copy = lax.axis_index("exp") % plan.copies
        gatt_recv = lax.dynamic_slice_in_dim(gatt_recv, copy * plan.blocks, plan.blocks, 0)
    gatt_rows = gatt_recv.reshape(plan.queries, plan.gw)

    gx, gw, small = call(
        backward_kernel,
        plan,
        [
            whole(x_all.shape), whole(wp.shape), whole(head_rows.shape), whole(spread.shape),
            whole(qkv.shape), whole(att.shape), whole(gatt_rows.shape), whole(lse.shape),
            whole(table.shape), whole(part.shape),
        ],
        [
            shaped(plan.exp, tok, width),
            shaped(width, plan.qkv),
            shaped(width, plan.chunk),
        ],
        [
            pltpu.VMEM((plan.length, 2 * plan.gw), f32),
            pltpu.VMEM((plan.length, plan.qkv), bf16),
            pltpu.VMEM((16, LANES), f32),
        ],
        name="backward",
    )(x_all, wp, head_rows, spread, qkv, att, gatt_rows, lse, table, part)

    gx_recv = along(gx)
    grad_tokens = call(
        finish_kernel,
        plan,
        [whole(gx_recv.shape), whole(grad_residual.shape), whole(x.shape), chunk_spec(plan)],
        [shaped(tok, width, dtype=f32)],
        name="finish",
    )(gx_recv, grad_residual, x, wp)[0]

    terms = jnp.concatenate([gwo, small, gw], axis=1).reshape(experts, plan.ffn, shard, -1)
    kept = lax.dynamic_index_in_dim(terms, ffn_index, 1, keepdims=False)
    given = lax.dynamic_index_in_dim(terms, plan.ffn - 1 - ffn_index, 1, keepdims=False)
    joined = (kept.astype(f32) + partner(given).astype(f32)).astype(bf16)
    got = exchange(joined)
    weight = shaped(shard, width, dtype=f32)
    gq, gk, gv, grad_w_output, sums = call(
        unpack_kernel,
        plan,
        [whole(got.shape)],
        [weight] * 4 + [shaped(shard, plan.chunk, dtype=f32)],
        name="unpack",
    )(got)
    return (
        output[None],
        grad_tokens[None],
        gq,
        gk,
        gv,
        grad_w_output,
        sums[:, experts : experts + 2].T,
        sums[: plan.bias_shard, experts + 2],
        sums[:, :experts],
        grad_w_in,
        grad_w_out,
    )


def solution(mesh):
    rows = P(("seq", "ffn"), "exp", None)
    shard = P(("seq", "exp", "ffn"), None)
    gains = P(None, ("seq", "exp", "ffn"))
    bias = P(("seq", "exp", "ffn"))
    hidden_last = P(("seq", "exp"), None, "ffn")
    hidden_first = P(("seq", "exp"), "ffn", None)
    return jax.shard_map(
        body,
        mesh=mesh,
        in_specs=(
            rows, rows, shard, shard, shard, shard, gains, bias, shard, hidden_last, hidden_first, rows,
        ),
        out_specs=(
            rows, rows, shard, shard, shard, shard, gains, bias, shard, hidden_last, hidden_first,
        ),
        check_vma=False,
    )
```
